32 devices in a mesh: row: 4 (over y, x), col: 8 (over z, core).
Axes of the slice: x: 2, y: 2, z: 4, core: 2. Of those that a mesh axis runs over, the one named last changes fastest.
Arguments:
- slab: bfloat16 [1024, 16384], P(('row', 'col')), may hold values from -0.1875 to 0.1875
- block_mask: int32 [32, 16], P(('row', 'col')), may hold values 0 or 1
- damping: float32 [16384], replicated, may hold values from 0.05 to 2
Outputs:
- hessian: float32 [16384, 16384], P('row', 'col')
The draws below stay inside these ranges and needn't reach their ends.
All inputs are finite; a program needn't handle non-finite values. No bound on the sum of `block_mask` on one device may be relied on, other than what follows from the above.
Results may differ from the reference program's by a relative error of at most 0.0003.
Values may be sent and summed in bfloat16 or wider, within the bound.
No kernel may reach another device: no remote copies, remote signals or barrier semaphores. Data moves between devices by JAX's collectives and lax.ppermute only.
A program may use at most 128 MiB of HBM per device.

```python
import math
import jax
import jax.numpy as jnp

P_SIZE = 16384
PB = 16
R_DEV = 32
GROUPS = 32
ROWS = 1024


def set_ends(entries, key, low, largest):
    dims = entries.shape
    spot = [jax.random.randint(jax.random.fold_in(key, axis), (), 0, dims[axis]) for axis in range(len(dims))]
    entries = entries.at[tuple(spot)].set(low)
    longest = dims.index(max(dims))
    spot[longest] = (spot[longest] + 1) % dims[longest]
    return entries.at[tuple(spot)].set(largest)


def level_of(stream_key, dims, pieces, least, largest):
    level = 1.0
    for axis_at, blocks in pieces:
        steps = jax.random.uniform(jax.random.fold_in(jax.random.fold_in(stream_key, 6), axis_at), (blocks,), jnp.float32, least / len(pieces), largest / len(pieces))
        level = level * jnp.repeat(jnp.exp(steps), dims[axis_at] // blocks).reshape((-1,) + (1,) * (len(dims) - 1 - axis_at))
    return level


def normal_values(rng, shape, scale, limit, pieces=(), kind=jnp.bfloat16):
    gain = level_of(rng, shape, pieces, -0.22, 0.18) if pieces else 1.0
    values = jax.random.normal(rng, shape, jnp.float32) * scale * gain
    return jnp.minimum(jnp.maximum(values, -limit), limit).astype(kind)


def setup_inputs(seed: int = 0) -> dict:
    seeds = jax.random.split(jax.random.key(seed), 4)
    return {
        "slab": normal_values(seeds[0], (ROWS, P_SIZE), ROWS ** -0.5, 0.1875, ((0, 32),)),
        "block_mask": set_ends((jax.random.randint(seeds[1], (GROUPS, PB), 0, 4) < 3).astype(jnp.int32), jax.random.fold_in(seeds[1], 1), 0, 1),
        "damping": jnp.clip(jnp.exp(jax.random.uniform(seeds[2], (P_SIZE,), jnp.float32, math.log(0.05), math.log(2.0))), 0.05, 2.0),
    }


def reference(slab, block_mask, damping):
    block_count = block_mask.shape[1]
    width = slab.shape[1]
    row_mask = jnp.repeat(block_mask, R_DEV, axis=0)
    full_mask = jnp.repeat(row_mask, width // block_count, axis=1).astype(slab.dtype)
    masked = slab * full_mask
    hessian = jnp.dot(masked.T, masked, preferred_element_type=jnp.float32)
    positions = jnp.arange(width, dtype=jnp.int32)
    return hessian.at[positions, positions].add(damping)
```

```python
import functools
import math

import jax
import jax.numpy as jnp
from jax import lax
from jax.experimental import pallas as pl
from jax.experimental.pallas import tpu as pltpu
from jax.sharding import PartitionSpec as P

AXES = ("row", "col")
CORES = 2
CHUNKS = (20, 12)
BLOCK_ROWS = 512


def pick_kernel(place, mask, slab, *outs):
    blocks = mask.shape[0]
    span = slab.shape[1] // blocks
    for slot, out in enumerate(outs):
        width = out.shape[1]
        step = min(width, span)
        for part in range(width // step):
            start = place[slot] * width + part * step
            start = pl.multiple_of(start, step)
            keep = mask[start // span].astype(jnp.float32)
            piece = slab[:, pl.ds(start, step)].astype(jnp.float32)
            out[:, part * step : (part + 1) * step] = (piece * keep).astype(out.dtype)


def pick_panels(slab, mask, place, width):
    count = place.shape[0]
    rows = slab.shape[0]
    return pl.pallas_call(
        pick_kernel,
        out_shape=[jax.ShapeDtypeStruct((rows, width), slab.dtype)] * count,
        in_specs=[
            pl.BlockSpec(memory_space=pltpu.SMEM),
            pl.BlockSpec(memory_space=pltpu.SMEM),
            pl.BlockSpec(memory_space=pltpu.VMEM),
        ],
        out_specs=[pl.BlockSpec(memory_space=pltpu.VMEM)] * count,
        name="pick_panels",
    )(place, mask, slab)


def product_kernel(count, first, aliased, where, col, damp, *refs):
    parts = refs[:count]
    out = refs[-1]
    step = pl.program_id(0)
    rows, cols = out.shape
    left = jnp.concatenate([part[...] for part in parts], axis=0)
    out[...] = lax.dot_general(
        left, col[...], (((0,), (0,)), ((), ())), preferred_element_type=jnp.float32
    )
    row_at = where[0] + first + step * rows
    col_at = where[1]

    @pl.when((row_at < col_at + cols) & (col_at < row_at + rows))
    def _():
        row_ids = lax.broadcasted_iota(jnp.int32, (rows, cols), 0) + row_at
        col_ids = lax.broadcasted_iota(jnp.int32, (rows, cols), 1) + col_at
        out[...] += jnp.where(row_ids == col_ids, damp[...], 0.0)


def product(parts, col, damp, where, total, first, block):
    depth, width = parts[0].shape
    rows = math.gcd(BLOCK_ROWS, width, first)
    steps = width // rows
    held, cols = col.shape
    count = len(parts)
    grid_spec = pltpu.PrefetchScalarGridSpec(
        num_scalar_prefetch=1,
        grid=(steps,),
        in_specs=[
            pl.BlockSpec((held, cols), lambda i, w: (0, 0)),
            pl.BlockSpec((1, cols), lambda i, w: (0, 0)),
        ]
        + [pl.BlockSpec((depth, rows), lambda i, w: (0, i))] * count
        + ([] if block is None else [pl.BlockSpec(memory_space=pl.ANY)]),
        out_specs=pl.BlockSpec((rows, cols), lambda i, w: (first // rows + i, 0)),
    )
    return pl.pallas_call(
        functools.partial(product_kernel, count, first, block is not None),
        out_shape=jax.ShapeDtypeStruct((total, cols), jnp.float32),
        grid_spec=grid_spec,
        input_output_aliases={} if block is None else {3 + count: 0},
        compiler_params=pltpu.CompilerParams(vmem_limit_bytes=40 << 20),
        cost_estimate=pl.CostEstimate(
            flops=2 * held * width * cols,
            bytes_accessed=2 * held * (width + cols) + 4 * width * cols,
            transcendentals=0,
        ),
        name="product",
    )(where, col, damp, *parts, *([] if block is None else [block]))


def shards(slab, block_mask, damping):
    lines = lax.axis_size("row")
    cols = lax.axis_size("col")
    planes = cols // CORES
    group, width = slab.shape
    panel = width // lines
    half = width // cols
    line = lax.axis_index("row")
    place = lax.axis_index("col")
    plane = place // CORES
    core = place % CORES

    def send(value, pairs):
        flat = []
        for (r0, q0, c0), (r1, q1, c1) in pairs:
            flat.append(((r0 * planes + q0) * CORES + c0, (r1 * planes + q1) * CORES + c1))
        return lax.ppermute(value, AXES, flat)

    everyone = [(r, q, c) for r in range(lines) for q in range(planes) for c in range(CORES)]

    def across_lines(value, m):
        return send(value, [((r, q, c), (r ^ m, q, c)) for r, q, c in everyone])

    def across_planes(value, k):
        return send(value, [((r, q, c), (r, q ^ k, c)) for r, q, c in everyone])

    def across_cores(value):
        return send(value, [((r, q, c), (r, q, 1 - c)) for r, q, c in everyone])

    order = [line ^ m for m in range(lines)] + [plane ^ k for k in range(planes)]
    picked = pick_panels(slab, block_mask[0], jnp.stack(order).astype(jnp.int32), panel)
    by_line, by_plane = picked[:lines], picked[lines:]

    row_parts = [by_line[0]] + [across_lines(by_line[m], m) for m in range(1, lines)]
    col_parts = [by_plane[0]] + [across_planes(by_plane[k], k) for k in range(1, planes)]

    mine = jnp.concatenate(col_parts, axis=0)
    col_lines = [mine] + [across_lines(mine, m) for m in range(1, lines)]
    stacked = jnp.stack(col_lines).reshape(lines, planes, group, panel)
    stacked = jnp.transpose(stacked, (1, 0, 2, 3)).reshape(lines * planes * group, panel)
    keep = lax.dynamic_slice_in_dim(stacked, core * half, half, 1)
    give = lax.dynamic_slice_in_dim(stacked, (1 - core) * half, half, 1)
    col_panel = jnp.concatenate([keep, across_cores(give)], axis=0)

    where = jnp.stack([line * panel, place * half]).astype(jnp.int32)
    damp = lax.dynamic_slice_in_dim(damping, place * half, half, 0)[None, :]

    share = panel // sum(CHUNKS)
    out = None
    first = 0
    for chunk in CHUNKS:
        size = chunk * share
        own = jnp.concatenate([p[:, first : first + size] for p in row_parts], axis=0)
        parts = [own]
        if planes == 4:
            near = across_planes(own, 1)
            far = across_planes(own, 2)
            mid = send(own, [((r, q, c), (r, q ^ 3, c)) for r, q, c in everyone if q in (1, 2)])
            pairs = [((r, q, c), (r, q ^ 1, c)) for r, q, c in everyone if q in (1, 2)]
            last = send(far, pairs)
            parts += [near, far, jnp.where((plane == 1) | (plane == 2), mid, last)]
        else:
            parts += [across_planes(own, k) for k in range(1, planes)]
        parts += [across_cores(p) for p in parts]
        out = product(parts, col_panel, damp, where, panel, first, out)
        first += size
    return out


def solution(mesh):
    placed = (P(("row", "col"), None), P(("row", "col"), None), P())
    return jax.shard_map(
        shards, mesh=mesh, in_specs=placed, out_specs=P("row", "col"), check_vma=False
    )
```

```python
import functools
import math

import jax
import jax.numpy as jnp
from jax import lax
from jax.experimental import pallas as pl
from jax.experimental.pallas import tpu as pltpu
from jax.sharding import PartitionSpec as P

AXES = ("row", "col")
CORES = 2
CHUNKS = (16, 16)
BLOCK_ROWS = 512


def after(value, *others):
    return lax.optimization_barrier((value,) + others)[0]


def pick_kernel(lines, mask, slab, *outs):
    line = lax.axis_index("row")
    plane = lax.axis_index("col") // CORES
    span = slab.shape[1] // mask.shape[1]
    for slot, out in enumerate(outs):
        width = out.shape[1]
        step = min(width, span)
        panel = line ^ slot if slot < lines else plane ^ (slot - lines)
        for part in range(width // step):
            start = pl.multiple_of(panel * width + part * step, step)
            keep = mask[0, start // span]
            piece = slab[:, pl.ds(start, step)]
            out[:, part * step : (part + 1) * step] = jnp.where(keep != 0, piece, jnp.zeros_like(piece))


def pick_panels(slab, mask, lines, planes):
    rows, width = slab.shape
    return pl.pallas_call(
        functools.partial(pick_kernel, lines),
        out_shape=[jax.ShapeDtypeStruct((rows, width // lines), slab.dtype)] * (lines + planes),
        in_specs=[
            pl.BlockSpec(memory_space=pltpu.SMEM),
            pl.BlockSpec(memory_space=pltpu.VMEM),
        ],
        out_specs=[pl.BlockSpec(memory_space=pltpu.VMEM)] * (lines + planes),
        name="pick_panels",
    )(mask, slab)


def product_kernel(count, lines, total, first, col, damp, *refs):
    parts = refs[:count]
    out = refs[-1]
    step = pl.program_id(0)
    rows, cols = out.shape
    group = parts[0].shape[0] // lines
    left = jnp.concatenate(
        [part[m * group : (m + 1) * group, :] for m in range(lines) for part in parts], axis=0
    )
    out[...] = lax.dot_general(
        left, col[...], (((0,), (0,)), ((), ())), preferred_element_type=jnp.float32
    )
    row_at = lax.axis_index("row") * total + first + step * rows
    col_at = lax.axis_index("col") * cols

    @pl.when((row_at < col_at + cols) & (col_at < row_at + rows))
    def _():
        row_ids = lax.broadcasted_iota(jnp.int32, (rows, cols), 0) + row_at
        col_ids = lax.broadcasted_iota(jnp.int32, (rows, cols), 1) + col_at
        mine = damp[:, pl.ds(pl.multiple_of(col_at, cols), cols)]
        out[...] += jnp.where(row_ids == col_ids, mine, 0.0)


def product(parts, col, damp, lines, total, first, width, block):
    depth = parts[0].shape[0]
    rows = math.gcd(BLOCK_ROWS, width, first)
    steps = width // rows
    held, cols = col.shape
    count = len(parts)
    return pl.pallas_call(
        functools.partial(product_kernel, count, lines, total, first),
        out_shape=jax.ShapeDtypeStruct((total, cols), jnp.float32),
        grid=(steps,),
        in_specs=[
            pl.BlockSpec((held, cols), lambda i: (0, 0)),
            pl.BlockSpec(damp.shape, lambda i: (0, 0)),
        ]
        + [
            pl.BlockSpec((depth, rows), lambda i, at=first // rows if p.shape[1] == total else 0: (0, at + i))
            for p in parts
        ]
        + ([] if block is None else [pl.BlockSpec(memory_space=pl.ANY)]),
        out_specs=pl.BlockSpec((rows, cols), lambda i: (first // rows + i, 0)),
        input_output_aliases={} if block is None else {2 + count: 0},
        compiler_params=pltpu.CompilerParams(vmem_limit_bytes=40 << 20),
        cost_estimate=pl.CostEstimate(flops=0, bytes_accessed=0, transcendentals=0),
        name="product",
    )(col, damp, *parts, *([] if block is None else [block]))


def shards(slab, block_mask, damping):
    lines = lax.axis_size("row")
    cols = lax.axis_size("col")
    planes = cols // CORES
    group, width = slab.shape
    panel = width // lines
    half = width // cols
    line = lax.axis_index("row")
    place = lax.axis_index("col")
    plane = place // CORES
    core = place % CORES

    everyone = [(r, q, c) for r in range(lines) for q in range(planes) for c in range(CORES)]

    def send(value, to):
        flat = []
        for r, q, c in everyone:
            target = to(r, q, c)
            if target is not None:
                r1, q1, c1 = target
                flat.append(((r * planes + q) * CORES + c, (r1 * planes + q1) * CORES + c1))
        return lax.ppermute(value, AXES, flat)

    def across_lines(value, m):
        return send(value, lambda r, q, c: (r ^ m, q, c))

    def across_planes(value, k):
        return send(value, lambda r, q, c: (r, q ^ k, c))

    def across_cores(value):
        return send(value, lambda r, q, c: (r, q, 1 - c))

    def swap_inner(value):
        return send(value, lambda r, q, c: (r, q ^ 3, c) if q in (1, 2) else None)

    def push_out(value):
        return send(value, lambda r, q, c: (r, q ^ 1, c) if q in (1, 2) else None)

    picked = pick_panels(slab, block_mask, lines, planes)
    by_line, by_plane = picked[:lines], picked[lines:]

    row_parts = [by_line[0]] + [across_lines(by_line[m], m) for m in range(1, lines)]
    col_parts = [by_plane[0]]
    for k in range(1, planes):
        col_parts.append(across_planes(after(by_plane[k], row_parts[1]) if k == 1 else by_plane[k], k))
    mine = jnp.concatenate(col_parts, axis=0)
    keep = lax.dynamic_slice_in_dim(mine, core * half, half, 1)
    give = lax.dynamic_slice_in_dim(mine, (1 - core) * half, half, 1)
    mine = jnp.concatenate([keep, across_cores(give)], axis=0)
    own = jnp.concatenate(row_parts, axis=0)

    share = panel // sum(CHUNKS)
    cuts = [0]
    for chunk in CHUNKS:
        cuts.append(cuts[-1] + chunk * share)

    def cut(value):
        return [value[:, i:j] for i, j in zip(cuts, cuts[1:])]

    if planes == 4 and lines == 4:
        inner = (plane == 1) | (plane == 2)
        near = across_planes(own, 1)
        mid = swap_inner(own)
        col_lines = [mine, across_lines(mine, 1), across_lines(mine, 2)]
        one, two = col_lines[1:]
        near, mid = lax.optimization_barrier((near, mid))
        far_in = swap_inner(near)
        far_out = push_out(mid)
        third = across_lines(after(mine, near, mid, one, two), 3)
        held = jnp.concatenate([mine, one, two], axis=0)
        far_in, far_out, third, held = lax.optimization_barrier((far_in, far_out, third, held))
        col_panel = jnp.concatenate([held, third], axis=0)
        last = []
        for piece in cut(far_in):
            last.append(push_out(after(piece, *last, *([col_panel] if last else []))))
        far = jnp.where(inner, far_in, far_out)
        across = [across_cores(p) for p in (own, near, far)]
        split = list(zip(cut(mid), last))
        full = [own, near, far] + across
    else:
        col_lines = [mine] + [across_lines(mine, m) for m in range(1, lines)]
        full = [own] + [across_planes(own, k) for k in range(1, planes)]
        full += [across_cores(p) for p in full]
        split = [None] * len(CHUNKS)
        col_panel = jnp.concatenate(col_lines, axis=0)

    out = None
    for first, end, pair in zip(cuts, cuts[1:], split):
        parts = full
        if pair is not None:
            middle, outer = pair
            if out is not None:
                outer, out = lax.optimization_barrier((outer, out))
            part = jnp.where(inner, middle, outer)
            at = len(full) // 2
            parts = full[:at] + [part] + full[at:] + [across_cores(part)]
        out = product(parts, col_panel, damping[None, :], lines, panel, first, end - first, out)
    return out


def solution(mesh):
    placed = (P(("row", "col"), None), P(("row", "col"), None), P())
    return jax.shard_map(
        shards, mesh=mesh, in_specs=placed, out_specs=P("row", "col"), check_vma=False
    )
```

```python
import functools
import math

import jax
import jax.numpy as jnp
from jax import lax
from jax.experimental import pallas as pl
from jax.experimental.pallas import tpu as pltpu
from jax.sharding import PartitionSpec as P

AXES = ("row", "col")
CORES = 2
CHUNKS = (16, 16)
BLOCK_ROWS = 512


def after(value, *others):
    return lax.optimization_barrier((value,) + others)[0]


def pick_kernel(lines, mask, slab, *outs):
    line = lax.axis_index("row")
    plane = lax.axis_index("col") // CORES
    span = slab.shape[1] // mask.shape[1]
    for slot, out in enumerate(outs):
        width = out.shape[1]
        step = min(width, span)
        panel = line ^ slot if slot < lines else plane ^ (slot - lines)
        for part in range(width // step):
            start = pl.multiple_of(panel * width + part * step, step)
            keep = mask[0, start // span]
            piece = slab[:, pl.ds(start, step)]
            out[:, part * step : (part + 1) * step] = jnp.where(keep != 0, piece, jnp.zeros_like(piece))


def pick_panels(slab, mask, lines, planes):
    rows, width = slab.shape
    return pl.pallas_call(
        functools.partial(pick_kernel, lines),
        out_shape=[jax.ShapeDtypeStruct((rows, width // lines), slab.dtype)] * (lines + planes),
        in_specs=[
            pl.BlockSpec(memory_space=pltpu.SMEM),
            pl.BlockSpec(memory_space=pltpu.VMEM),
        ],
        out_specs=[pl.BlockSpec(memory_space=pltpu.VMEM)] * (lines + planes),
        name="pick_panels",
    )(mask, slab)


def product_kernel(picks, lines, total, first, col, damp, *refs):
    out = refs[-1]
    step = pl.program_id(0)
    rows, cols = out.shape
    plane = lax.axis_index("col") // CORES
    inner = (plane == 1) | (plane == 2)
    slots = []
    for pick in picks:
        value = refs[pick[0]][...]
        if len(pick) == 2:
            value = jnp.where(inner, value, refs[pick[1]][...])
        slots.append(value)
    group = slots[0].shape[0] // lines
    left = jnp.concatenate(
        [slot[m * group : (m + 1) * group, :] for m in range(lines) for slot in slots], axis=0
    )
    out[...] = lax.dot_general(
        left, col[...], (((0,), (0,)), ((), ())), preferred_element_type=jnp.float32
    )
    row_at = lax.axis_index("row") * total + first + step * rows
    col_at = lax.axis_index("col") * cols

    @pl.when((row_at < col_at + cols) & (col_at < row_at + rows))
    def _():
        row_ids = lax.broadcasted_iota(jnp.int32, (rows, cols), 0) + row_at
        col_ids = lax.broadcasted_iota(jnp.int32, (rows, cols), 1) + col_at
        mine = damp[:, pl.ds(pl.multiple_of(col_at, cols), cols)]
        out[...] += jnp.where(row_ids == col_ids, mine, 0.0)


def product(slots, col, damp, lines, total, first, width, block):
    parts, picks = [], []
    for slot in slots:
        picks.append(tuple(range(len(parts), len(parts) + len(slot))))
        parts.extend(slot)
    depth = parts[0].shape[0]
    rows = math.gcd(BLOCK_ROWS, width, first)
    steps = width // rows
    held, cols = col.shape
    count = len(parts)
    return pl.pallas_call(
        functools.partial(product_kernel, picks, lines, total, first),
        out_shape=jax.ShapeDtypeStruct((total, cols), jnp.float32),
        grid=(steps,),
        in_specs=[
            pl.BlockSpec((held, cols), lambda i: (0, 0)),
            pl.BlockSpec(damp.shape, lambda i: (0, 0)),
        ]
        + [
            pl.BlockSpec((depth, rows), lambda i, at=first // rows if p.shape[1] == total else 0: (0, at + i))
            for p in parts
        ]
        + ([] if block is None else [pl.BlockSpec(memory_space=pl.ANY)]),
        out_specs=pl.BlockSpec((rows, cols), lambda i: (first // rows + i, 0)),
        input_output_aliases={} if block is None else {2 + count: 0},
        compiler_params=pltpu.CompilerParams(vmem_limit_bytes=40 << 20),
        cost_estimate=pl.CostEstimate(flops=0, bytes_accessed=0, transcendentals=0),
        name="product",
    )(col, damp, *parts, *([] if block is None else [block]))


def shards(slab, block_mask, damping):
    lines = lax.axis_size("row")
    cols = lax.axis_size("col")
    planes = cols // CORES
    group, width = slab.shape
    panel = width // lines
    half = width // cols
    line = lax.axis_index("row")
    place = lax.axis_index("col")
    plane = place // CORES
    core = place % CORES

    everyone = [(r, q, c) for r in range(lines) for q in range(planes) for c in range(CORES)]

    def send(value, to):
        flat = []
        for r, q, c in everyone:
            target = to(r, q, c)
            if target is not None:
                r1, q1, c1 = target
                flat.append(((r * planes + q) * CORES + c, (r1 * planes + q1) * CORES + c1))
        return lax.ppermute(value, AXES, flat)

    def across_lines(value, m):
        return send(value, lambda r, q, c: (r ^ m, q, c))

    def across_planes(value, k):
        return send(value, lambda r, q, c: (r, q ^ k, c))

    def across_cores(value):
        return send(value, lambda r, q, c: (r, q, 1 - c))

    def swap_inner(value):
        return send(value, lambda r, q, c: (r, q ^ 3, c) if q in (1, 2) else None)

    def push_out(value):
        return send(value, lambda r, q, c: (r, q ^ 1, c) if q in (1, 2) else None)

    picked = pick_panels(slab, block_mask, lines, planes)
    by_line, by_plane = picked[:lines], picked[lines:]

    col_parts = [by_plane[0]] + [across_planes(by_plane[k], k) for k in range(planes - 1, 0, -1)][::-1]
    row_parts = [by_line[0]]
    for m in range(1, lines):
        row_parts.append(across_lines(after(by_line[m], *row_parts[1:2]) if m == 3 else by_line[m], m))
    mine = jnp.concatenate(col_parts, axis=0)
    keep = lax.dynamic_slice_in_dim(mine, core * half, half, 1)
    give = lax.dynamic_slice_in_dim(mine, (1 - core) * half, half, 1)
    mine = jnp.concatenate([keep, across_cores(give)], axis=0)
    own = jnp.concatenate(row_parts, axis=0)

    share = panel // sum(CHUNKS)
    cuts = [0]
    for chunk in CHUNKS:
        cuts.append(cuts[-1] + chunk * share)

    def cut(value):
        return [value[:, i:j] for i, j in zip(cuts, cuts[1:])]

    if planes == 4 and lines == 4:
        inner = (plane == 1) | (plane == 2)
        near = across_planes(own, 1)
        mid = swap_inner(own)
        col_lines = [mine, across_lines(mine, 1), across_lines(mine, 2)]
        one, two = col_lines[1:]
        near, mid = lax.optimization_barrier((near, mid))
        far_in = swap_inner(near)
        far_out = push_out(mid)
        third = across_lines(mine, 3)
        first_own = after(cut(own)[0], near, mid)
        direct = send(first_own, lambda r, q, c: (r, q ^ 3, c) if q in (0, 3) else None)
        held = jnp.concatenate([mine, one, two], axis=0)
        col_panel = jnp.concatenate([held, third], axis=0)
        far_in, far_out, col_panel, direct = lax.optimization_barrier(
            (far_in, far_out, col_panel, direct)
        )
        last = [direct, push_out(cut(far_in)[1])]
        far = jnp.where(inner, far_in, far_out)
        slots = [[p] for p in (own, near, far, mid)]
    else:
        col_lines = [mine] + [across_lines(mine, m) for m in range(1, lines)]
        col_panel = jnp.concatenate(col_lines, axis=0)
        slots = [[own]] + [[across_planes(own, k)] for k in range(1, planes)]
        last = [None] * len(CHUNKS)

    sides = [[across_cores(p) for p in slot] for slot in slots]
    out = None
    for first, end, outer in zip(cuts, cuts[1:], last):
        ours, theirs = slots, sides
        if outer is not None:
            if out is not None:
                outer, out = lax.optimization_barrier((outer, out))
            ours = slots[:3] + [slots[3] + [outer]]
            theirs = sides[:3] + [sides[3] + [across_cores(outer)]]
        out = product(ours + theirs, col_panel, damping[None, :], lines, panel, first, end - first, out)
    return out


def solution(mesh):
    placed = (P(("row", "col"), None), P(("row", "col"), None), P())
    return jax.shard_map(
        shards, mesh=mesh, in_specs=placed, out_specs=P("row", "col"), check_vma=False
    )
```

```python
import functools
import math

import jax
import jax.numpy as jnp
from jax import lax
from jax.experimental import pallas as pl
from jax.experimental.pallas import tpu as pltpu
from jax.sharding import PartitionSpec as P

AXES = ("row", "col")
CORES = 2
CHUNKS = (16, 16)
BLOCK_ROWS = 512


def after(value, *others):
    return lax.optimization_barrier((value,) + others)[0]


def pick_kernel(lines, mask, slab, *outs):
    line = lax.axis_index("row")
    plane = lax.axis_index("col") // CORES
    span = slab.shape[1] // mask.shape[1]
    for slot, out in enumerate(outs):
        width = out.shape[1]
        step = min(width, span)
        panel = line ^ slot if slot < lines else plane ^ (slot - lines)
        for part in range(width // step):
            start = pl.multiple_of(panel * width + part * step, step)
            keep = mask[0, start // span]
            piece = slab[:, pl.ds(start, step)]
            out[:, part * step : (part + 1) * step] = jnp.where(keep != 0, piece, jnp.zeros_like(piece))


def pick_panels(slab, mask, lines, planes):
    rows, width = slab.shape
    return pl.pallas_call(
        functools.partial(pick_kernel, lines),
        out_shape=[jax.ShapeDtypeStruct((rows, width // lines), slab.dtype)] * (lines + planes),
        in_specs=[
            pl.BlockSpec(memory_space=pltpu.SMEM),
            pl.BlockSpec(memory_space=pltpu.VMEM),
        ],
        out_specs=[pl.BlockSpec(memory_space=pltpu.VMEM)] * (lines + planes),
        name="pick_panels",
    )(mask, slab)


def product_kernel(picks, lines, total, first, col, damp, *refs):
    out = refs[-1]
    step = pl.program_id(0)
    rows, cols = out.shape
    plane = lax.axis_index("col") // CORES
    inner = (plane == 1) | (plane == 2)
    slots = []
    for pick in picks:
        value = refs[pick[0]][...]
        if len(pick) == 2:
            value = jnp.where(inner, value, refs[pick[1]][...])
        slots.append(value)
    group = slots[0].shape[0] // lines
    left = jnp.concatenate(
        [slot[m * group : (m + 1) * group, :] for m in range(lines) for slot in slots], axis=0
    )
    out[...] = lax.dot_general(
        left, col[...], (((0,), (0,)), ((), ())), preferred_element_type=jnp.float32
    )
    row_at = lax.axis_index("row") * total + first + step * rows
    col_at = lax.axis_index("col") * cols

    @pl.when((row_at < col_at + cols) & (col_at < row_at + rows))
    def _():
        row_ids = lax.broadcasted_iota(jnp.int32, (rows, cols), 0) + row_at
        col_ids = lax.broadcasted_iota(jnp.int32, (rows, cols), 1) + col_at
        mine = damp[:, pl.ds(pl.multiple_of(col_at, cols), cols)]
        out[...] += jnp.where(row_ids == col_ids, mine, 0.0)


def product(slots, col, damp, lines, total, first, width, block):
    parts, picks = [], []
    for slot in slots:
        picks.append(tuple(range(len(parts), len(parts) + len(slot))))
        parts.extend(slot)
    depth = parts[0].shape[0]
    rows = math.gcd(BLOCK_ROWS, width, first)
    steps = width // rows
    held, cols = col.shape
    count = len(parts)
    return pl.pallas_call(
        functools.partial(product_kernel, picks, lines, total, first),
        out_shape=jax.ShapeDtypeStruct((total, cols), jnp.float32),
        grid=(steps,),
        in_specs=[
            pl.BlockSpec((held, cols), lambda i: (0, 0)),
            pl.BlockSpec(damp.shape, lambda i: (0, 0)),
        ]
        + [
            pl.BlockSpec((depth, rows), lambda i, at=first // rows if p.shape[1] == total else 0: (0, at + i))
            for p in parts
        ]
        + ([] if block is None else [pl.BlockSpec(memory_space=pl.ANY)]),
        out_specs=pl.BlockSpec((rows, cols), lambda i: (first // rows + i, 0)),
        input_output_aliases={} if block is None else {2 + count: 0},
        compiler_params=pltpu.CompilerParams(vmem_limit_bytes=28 << 20),
        cost_estimate=pl.CostEstimate(flops=0, bytes_accessed=0, transcendentals=0),
        name="product",
    )(col, damp, *parts, *([] if block is None else [block]))


def shards(slab, block_mask, damping):
    lines = lax.axis_size("row")
    cols = lax.axis_size("col")
    planes = cols // CORES
    group, width = slab.shape
    panel = width // lines
    half = width // cols
    line = lax.axis_index("row")
    place = lax.axis_index("col")
    plane = place // CORES
    core = place % CORES

    everyone = [(r, q, c) for r in range(lines) for q in range(planes) for c in range(CORES)]

    def send(value, to):
        flat = []
        for r, q, c in everyone:
            target = to(r, q, c)
            if target is not None:
                r1, q1, c1 = target
                flat.append(((r * planes + q) * CORES + c, (r1 * planes + q1) * CORES + c1))
        return lax.ppermute(value, AXES, flat)

    def across_lines(value, m):
        return send(value, lambda r, q, c: (r ^ m, q, c))

    def across_planes(value, k):
        return send(value, lambda r, q, c: (r, q ^ k, c))

    def across_cores(value):
        return send(value, lambda r, q, c: (r, q, 1 - c))

    def swap_inner(value):
        return send(value, lambda r, q, c: (r, q ^ 3, c) if q in (1, 2) else None)

    def push_out(value):
        return send(value, lambda r, q, c: (r, q ^ 1, c) if q in (1, 2) else None)

    picked = pick_panels(slab, block_mask, lines, planes)
    by_line, by_plane = picked[:lines], picked[lines:]

    col_parts = [by_plane[0]] + [across_planes(by_plane[k], k) for k in range(planes - 1, 0, -1)][::-1]
    row_parts = [by_line[0]]
    for m in range(1, lines):
        row_parts.append(across_lines(after(by_line[m], *row_parts[1:2]) if m == 3 else by_line[m], m))
    mine = jnp.concatenate(col_parts, axis=0)
    keep = lax.dynamic_slice_in_dim(mine, core * half, half, 1)
    give = lax.dynamic_slice_in_dim(mine, (1 - core) * half, half, 1)
    mine = jnp.concatenate([keep, across_cores(give)], axis=0)
    own = jnp.concatenate(row_parts, axis=0)

    share = panel // sum(CHUNKS)
    cuts = [0]
    for chunk in CHUNKS:
        cuts.append(cuts[-1] + chunk * share)

    def cut(value):
        return [value[:, i:j] for i, j in zip(cuts, cuts[1:])]

    if planes == 4 and lines == 4:
        near = across_planes(own, 1)
        mid = swap_inner(own)
        col_lines = [mine, across_lines(mine, 1), across_lines(mine, 2)]
        one, two = col_lines[1:]
        near, mid = lax.optimization_barrier((near, mid))
        far_in = swap_inner(near)
        far_out = push_out(mid)
        third = across_lines(mine, 3)
        first_own = after(cut(own)[0], near)
        direct = send(first_own, lambda r, q, c: (r, q ^ 3, c) if q in (0, 3) else None)
        held = jnp.concatenate(lax.optimization_barrier((mine, one, two)), axis=0)
        col_panel = jnp.concatenate([held, third], axis=0)
        far_in, far_out, col_panel, direct = lax.optimization_barrier(
            (far_in, far_out, col_panel, direct)
        )
        last = [direct, push_out(cut(far_in)[1])]
        slots = [[own], [near], [far_in, far_out], [mid]]
    else:
        col_lines = [mine] + [across_lines(mine, m) for m in range(1, lines)]
        col_panel = jnp.concatenate(col_lines, axis=0)
        slots = [[own]] + [[across_planes(own, k)] for k in range(1, planes)]
        last = [None] * len(CHUNKS)

    sides = [[across_cores(p) for p in slot] for slot in slots]
    out = None
    for first, end, outer in zip(cuts, cuts[1:], last):
        ours, theirs = slots, sides
        if outer is not None:
            if out is not None:
                outer, out = lax.optimization_barrier((outer, out))
            ours = slots[:3] + [slots[3] + [outer]]
            theirs = sides[:3] + [sides[3] + [across_cores(outer)]]
        out = product(ours + theirs, col_panel, damping[None, :], lines, panel, first, end - first, out)
    return out


def solution(mesh):
    placed = (P(("row", "col"), None), P(("row", "col"), None), P())
    return jax.shard_map(
        shards, mesh=mesh, in_specs=placed, out_specs=P("row", "col"), check_vma=False
    )
```

```python
import functools
import math

import jax
import jax.numpy as jnp
from jax import lax
from jax.experimental import pallas as pl
from jax.experimental.pallas import tpu as pltpu
from jax.sharding import PartitionSpec as P

AXES = ("row", "col")
CORES = 2
CHUNKS = (16, 16)
BLOCK_ROWS = 512


def after(value, *others):
    return lax.optimization_barrier((value,) + others)[0]


def pick_kernel(axis, mask, slab, *outs):
    place = lax.axis_index("row") if axis == "row" else lax.axis_index("col") // CORES
    span = slab.shape[1] // mask.shape[1]
    for slot, out in enumerate(outs):
        width = out.shape[1]
        step = min(width, span)
        panel = place ^ slot
        for part in range(width // step):
            start = pl.multiple_of(panel * width + part * step, step)
            keep = mask[0, start // span]
            piece = slab[:, pl.ds(start, step)]
            out[:, part * step : (part + 1) * step] = jnp.where(keep != 0, piece, jnp.zeros_like(piece))


def pick_panels(slab, mask, axis, count):
    rows, width = slab.shape
    return pl.pallas_call(
        functools.partial(pick_kernel, axis),
        out_shape=[jax.ShapeDtypeStruct((rows, width // count), slab.dtype)] * count,
        in_specs=[
            pl.BlockSpec(memory_space=pltpu.SMEM),
            pl.BlockSpec(memory_space=pltpu.VMEM),
        ],
        out_specs=[pl.BlockSpec(memory_space=pltpu.VMEM)] * count,
        name="pick_panels",
    )(mask, slab)


def product_kernel(picks, lines, total, first, col, damp, *refs):
    out = refs[-1]
    step = pl.program_id(0)
    rows, cols = out.shape
    plane = lax.axis_index("col") // CORES
    inner = (plane == 1) | (plane == 2)
    slots = []
    for pick in picks:
        value = refs[pick[0]][...]
        if len(pick) == 2:
            value = jnp.where(inner, value, refs[pick[1]][...])
        slots.append(value)
    group = slots[0].shape[0] // lines
    left = jnp.concatenate(
        [slot[m * group : (m + 1) * group, :] for m in range(lines) for slot in slots], axis=0
    )
    out[...] = lax.dot_general(
        left, col[...], (((0,), (0,)), ((), ())), preferred_element_type=jnp.float32
    )
    row_at = lax.axis_index("row") * total + first + step * rows
    col_at = lax.axis_index("col") * cols

    @pl.when((row_at < col_at + cols) & (col_at < row_at + rows))
    def _():
        row_ids = lax.broadcasted_iota(jnp.int32, (rows, cols), 0) + row_at
        col_ids = lax.broadcasted_iota(jnp.int32, (rows, cols), 1) + col_at
        mine = damp[:, pl.ds(pl.multiple_of(col_at, cols), cols)]
        out[...] += jnp.where(row_ids == col_ids, mine, 0.0)


def product(slots, col, damp, lines, total, first, width, block):
    parts, picks = [], []
    for slot in slots:
        picks.append(tuple(range(len(parts), len(parts) + len(slot))))
        parts.extend(slot)
    depth = parts[0].shape[0]
    rows = math.gcd(BLOCK_ROWS, width, first)
    steps = width // rows
    held, cols = col.shape
    count = len(parts)
    return pl.pallas_call(
        functools.partial(product_kernel, picks, lines, total, first),
        out_shape=jax.ShapeDtypeStruct((total, cols), jnp.float32),
        grid=(steps,),
        in_specs=[
            pl.BlockSpec((held, cols), lambda i: (0, 0)),
            pl.BlockSpec(damp.shape, lambda i: (0, 0)),
        ]
        + [
            pl.BlockSpec((depth, rows), lambda i, at=first // rows if p.shape[1] == total else 0: (0, at + i))
            for p in parts
        ]
        + ([] if block is None else [pl.BlockSpec(memory_space=pl.ANY)]),
        out_specs=pl.BlockSpec((rows, cols), lambda i: (first // rows + i, 0)),
        input_output_aliases={} if block is None else {2 + count: 0},
        compiler_params=pltpu.CompilerParams(vmem_limit_bytes=28 << 20),
        cost_estimate=pl.CostEstimate(flops=0, bytes_accessed=0, transcendentals=0),
        name="product",
    )(col, damp, *parts, *([] if block is None else [block]))


def shards(slab, block_mask, damping):
    lines = lax.axis_size("row")
    cols = lax.axis_size("col")
    planes = cols // CORES
    group, width = slab.shape
    panel = width // lines
    half = width // cols
    line = lax.axis_index("row")
    place = lax.axis_index("col")
    plane = place // CORES
    core = place % CORES

    everyone = [(r, q, c) for r in range(lines) for q in range(planes) for c in range(CORES)]

    def send(value, to):
        flat = []
        for r, q, c in everyone:
            target = to(r, q, c)
            if target is not None:
                r1, q1, c1 = target
                flat.append(((r * planes + q) * CORES + c, (r1 * planes + q1) * CORES + c1))
        return lax.ppermute(value, AXES, flat)

    def across_lines(value, m):
        return send(value, lambda r, q, c: (r ^ m, q, c))

    def across_planes(value, k):
        return send(value, lambda r, q, c: (r, q ^ k, c))

    def across_cores(value):
        return send(value, lambda r, q, c: (r, q, 1 - c))

    def swap_inner(value):
        return send(value, lambda r, q, c: (r, q ^ 3, c) if q in (1, 2) else None)

    def push_out(value):
        return send(value, lambda r, q, c: (r, q ^ 1, c) if q in (1, 2) else None)

    by_plane = pick_panels(slab, block_mask, "col", planes)
    by_line = pick_panels(after(slab, by_plane[0]), block_mask, "row", lines)

    col_parts = [by_plane[0]] + [across_planes(by_plane[k], k) for k in range(planes - 1, 0, -1)][::-1]
    row_parts = [by_line[0]]
    for m in range(1, lines):
        row_parts.append(across_lines(by_line[m], m))
    mine = jnp.concatenate(col_parts, axis=0)
    keep = lax.dynamic_slice_in_dim(mine, core * half, half, 1)
    give = lax.dynamic_slice_in_dim(mine, (1 - core) * half, half, 1)
    mine = jnp.concatenate([keep, across_cores(give)], axis=0)
    own = jnp.concatenate(row_parts, axis=0)

    share = panel // sum(CHUNKS)
    cuts = [0]
    for chunk in CHUNKS:
        cuts.append(cuts[-1] + chunk * share)

    def cut(value):
        return [value[:, i:j] for i, j in zip(cuts, cuts[1:])]

    if planes == 4 and lines == 4:
        near = across_planes(own, 1)
        mid = swap_inner(own)
        col_lines = [mine, across_lines(mine, 1), across_lines(mine, 2)]
        one, two = col_lines[1:]
        near, mid = lax.optimization_barrier((near, mid))
        far_in = swap_inner(near)
        far_out = push_out(mid)
        third = across_lines(mine, 3)
        first_own = after(cut(own)[0], near)
        direct = send(first_own, lambda r, q, c: (r, q ^ 3, c) if q in (0, 3) else None)
        held = jnp.concatenate(lax.optimization_barrier((mine, one, two)), axis=0)
        col_panel = jnp.concatenate([held, third], axis=0)
        far_in, far_out, col_panel, direct = lax.optimization_barrier(
            (far_in, far_out, col_panel, direct)
        )
        last = [direct, push_out(cut(far_in)[1])]
        slots = [[own], [near], [far_in, far_out], [mid]]
    else:
        col_lines = [mine] + [across_lines(mine, m) for m in range(1, lines)]
        col_panel = jnp.concatenate(col_lines, axis=0)
        slots = [[own]] + [[across_planes(own, k)] for k in range(1, planes)]
        last = [None] * len(CHUNKS)

    sides = [[across_cores(p) for p in slot] for slot in slots]
    out = None
    for first, end, outer in zip(cuts, cuts[1:], last):
        ours, theirs = slots, sides
        if outer is not None:
            if out is not None:
                outer, out = lax.optimization_barrier((outer, out))
            ours = slots[:3] + [slots[3] + [outer]]
            theirs = sides[:3] + [sides[3] + [across_cores(outer)]]
        out = product(ours + theirs, col_panel, damping[None, :], lines, panel, first, end - first, out)
    return out


def solution(mesh):
    placed = (P(("row", "col"), None), P(("row", "col"), None), P())
    return jax.shard_map(
        shards, mesh=mesh, in_specs=placed, out_specs=P("row", "col"), check_vma=False
    )
```
